32 devices in a mesh: atom: 8 (over y, x, core), mode: 4 (over z).
Axes of the slice: x: 2, y: 2, z: 4, core: 2. Of those that a mesh axis runs over, the one named last changes fastest.
Arguments:
- features: float32 [128, 8192], P(None, 'atom'), may hold values from -6 to 6
- positions: float32 [3, 8192], P(None, 'atom'), may hold values from 0 to 1, as said below
- wavevectors: int32 [3, 8192], P(None, 'mode'), may hold values from -384 to 384, as said below
- mode_filter: float32 [128, 8192], P(None, 'mode'), may hold values from -12 to 12
- radial_mix: float32 [4, 128, 128], replicated, may hold values from -0.03125 to 0.03125
- radial_rates: float32 [4], replicated, may hold values from 0.2 to 3
- neighbour_ids: int32 [64, 5], P(('atom', 'mode')), may hold values from 0 to 63, as said below
- live_counts: int32 [64], P(('atom', 'mode')), may hold values from 1 to 5, as said below
- cotangent: float32 [128, 8192], P(None, ('atom', 'mode')), may hold values from -6 to 6
Outputs:
- layer_out: float32 [128, 8192], P(None, ('atom', 'mode'))
- grad_features: float32 [128, 8192], P(None, ('atom', 'mode'))
- grad_filter: float32 [128, 8192], P(None, 'mode')
The draws below stay inside these ranges and needn't reach their ends.
Inputs may be any that keep to these rules, and one draw needn't show every extreme that they name: `positions`: row 0 of atom i lies between b / 64 and (b + 1) / 64, with b = i // 128; rows 1 and 2 lie anywhere in the range. `wavevectors`: row 0 lies between -384 and 384; rows 1 and 2 lie between -12 and 12. `neighbour_ids`: row b lists the 5 blocks (b + o) mod 64, o from -2 to 2, each once, in some order; only the first live_counts[b] slots are live. `live_counts`: some block has all 5 slots live.
All inputs are finite; a program needn't handle non-finite values.
Results may differ from the reference program's by a relative error of at most 0.00035.
Values sent between devices are 32-bit elements; how exact they have to be, the bound alone decides.
A program may use at most 128 MiB of HBM per device.

```python
import math
import jax
import jax.numpy as jnp
from jax import lax

C = 128
MODES = 8192
RADIAL = 4
BLOCK = 128
REACH = 2
ATOM_DEV = 1024
SLOTS = 5
ATOMS = 8192
NBLK = 64


def neighbour_plan(key):
    order_key = jax.random.fold_in(key, 11)
    first_key = jax.random.fold_in(key, 12)
    second_key = jax.random.fold_in(key, 13)
    shift_key = jax.random.fold_in(key, 14)
    scores = jax.random.randint(order_key, (NBLK, SLOTS), 0, 1000) * SLOTS + jnp.arange(SLOTS, dtype=jnp.int32)[None, :]
    ordering = jnp.argsort(scores, axis=1, stable=True).astype(jnp.int32)
    block_numbers = jnp.arange(NBLK, dtype=jnp.int32)
    neighbours = jnp.mod(block_numbers[:, None] + ordering - REACH, NBLK).astype(jnp.int32)
    first_draw = jax.random.randint(first_key, (NBLK,), 0, SLOTS)
    second_draw = jax.random.randint(second_key, (NBLK,), 0, SLOTS)
    shifted = jax.random.randint(shift_key, (), 0, NBLK)
    dense = jnp.mod(block_numbers + shifted, NBLK) < NBLK // 2
    counted = 1 + jnp.where(dense, jnp.maximum(first_draw, second_draw), jnp.minimum(first_draw, second_draw))
    counted = jnp.where(jnp.mod(block_numbers + shifted, NBLK) == 0, SLOTS, counted).astype(jnp.int32)
    return (neighbours, counted)


def draw_neighbour_ids(key, part):
    neighbours, counted = neighbour_plan(key)
    return neighbours


def draw_live_counts(key, part):
    neighbours, counted = neighbour_plan(key)
    return counted


def draw_wavevectors(key, part):
    long_key = jax.random.fold_in(key, 31)
    cross_key = jax.random.fold_in(key, 32)
    along = jax.random.randint(long_key, (1, MODES), -6 * NBLK, 6 * NBLK + 1)
    across = jax.random.randint(cross_key, (2, MODES), -12, 13)
    return jnp.concatenate([along, across], axis=0).astype(jnp.int32)


def draw_positions(key, part):
    inside_key = jax.random.fold_in(key, 21)
    cross_key = jax.random.fold_in(key, 22)
    inside = jax.random.uniform(inside_key, (ATOMS,), jnp.float32)
    cross = jax.random.uniform(cross_key, (2, ATOMS), jnp.float32)
    block_of = (jnp.arange(ATOMS, dtype=jnp.int32) // BLOCK).astype(jnp.float32)
    first_row = jnp.minimum((block_of + inside) / NBLK, 0.9999999)
    return jnp.concatenate([first_row[None, :], cross], axis=0).astype(jnp.float32)


def level_of(stream_key, dims, pieces, least, largest):
    factor_of = 1.0
    for dim, blocks in pieces:
        heights = jax.random.uniform(jax.random.fold_in(jax.random.fold_in(stream_key, 6), dim), (blocks,), jnp.float32, least / len(pieces), largest / len(pieces))
        factor_of = factor_of * jnp.repeat(jnp.exp(heights), dims[dim] // blocks).reshape((-1,) + (1,) * (len(dims) - 1 - dim))
    return factor_of


def bell_draw(key, dims, scale, bound, cuts=(), held_as=jnp.bfloat16):
    array = scale * jax.random.normal(key, dims, jnp.float32)
    if cuts:
        array = array * level_of(key, dims, cuts, -0.22, 0.18)
    return jnp.clip(array, -bound, bound).astype(held_as)


def setup_inputs(seed: int = 0) -> dict:
    key_list = jax.random.split(jax.random.key(seed), 10)
    return {
        "features": bell_draw(key_list[0], (C, ATOMS), 1.0, 6.0, ((1, 8),), jnp.float32),
        "positions": draw_positions(jax.random.fold_in(key_list[9], 71), 0),
        "wavevectors": draw_wavevectors(jax.random.fold_in(key_list[9], 71), 0),
        "mode_filter": bell_draw(key_list[3], (C, MODES), 2.0, 12.0, ((1, 4),), jnp.float32),
        "radial_mix": bell_draw(key_list[4], (RADIAL, C, C), (RADIAL * C * 64) ** -0.5, 0.03125, (), jnp.float32),
        "radial_rates": jnp.clip(jnp.exp(jax.random.uniform(key_list[5], (RADIAL,), jnp.float32, math.log(0.2), math.log(3.0))), 0.2, 3.0),
        "neighbour_ids": draw_neighbour_ids(jax.random.fold_in(key_list[9], 71), 0),
        "live_counts": draw_live_counts(jax.random.fold_in(key_list[9], 71), 0),
        "cotangent": bell_draw(key_list[8], (C, ATOMS), 1.0, 6.0, ((1, 32),), jnp.float32),
    }


def wave_tables(coords, wavevectors):
    wave_float = wavevectors.astype(jnp.float32)
    phases = 2.0 * jnp.pi * (coords[0][:, None] * wave_float[0][None, :] + coords[1][:, None] * wave_float[1][None, :] + coords[2][:, None] * wave_float[2][None, :])
    return jnp.cos(phases), jnp.sin(phases)


def pair_weights(own_coords, other_coords, radial_rates, total_blocks, live_mask):
    lengths = (total_blocks / jnp.pi, 2.0 / jnp.pi, 2.0 / jnp.pi)
    squared = None
    for axis_number in range(3):
        difference = own_coords[axis_number][:, None, :, None] - other_coords[axis_number][:, :, None, :]
        term = (lengths[axis_number] * jnp.sin(jnp.pi * difference)) ** 2
        squared = term if squared is None else squared + term
    return jnp.exp(-radial_rates[:, None, None, None, None] * squared[None]) * live_mask[None, :, :, None, None]


def matmul_exact(left, right):
    return jnp.dot(left, right, precision=lax.Precision.HIGHEST, preferred_element_type=jnp.float32)


def general_exact(left, right):
    return lax.dot_general(left, right, (((1,), (1,)), ((), ())), precision=lax.Precision.HIGHEST, preferred_element_type=jnp.float32)


def reference(features, positions, wavevectors, mode_filter, radial_mix, radial_rates, neighbour_ids, live_counts, cotangent):
    channels, atoms_total = features.shape
    inverse_count = 1.0 / atoms_total
    group_rows = ATOM_DEV
    group_count = atoms_total // group_rows
    feat_groups = features.reshape(channels, group_count, group_rows).transpose(1, 0, 2)
    cot_groups = cotangent.reshape(channels, group_count, group_rows).transpose(1, 0, 2)
    pos_groups = positions.reshape(3, group_count, group_rows).transpose(1, 0, 2)

    def accumulate(totals, inputs):
        feat_part, cot_part, pos_part = inputs
        cosines, sines = wave_tables(pos_part, wavevectors)
        return (totals[0] + matmul_exact(feat_part, cosines), totals[1] + matmul_exact(feat_part, sines), totals[2] + matmul_exact(cot_part, cosines), totals[3] + matmul_exact(cot_part, sines)), None

    zero_sums = jnp.zeros((channels, MODES), jnp.float32)
    sums, _ = lax.scan(accumulate, (zero_sums, zero_sums, zero_sums, zero_sums), (feat_groups, cot_groups, pos_groups))
    cos_sums, sin_sums, cot_cos, cot_sin = sums
    filt_cos = mode_filter * cos_sums * inverse_count
    filt_sin = mode_filter * sin_sums * inverse_count
    back_cos = mode_filter * cot_cos * inverse_count
    back_sin = mode_filter * cot_sin * inverse_count
    grad_filter = (cos_sums * cot_cos + sin_sums * cot_sin) * inverse_count

    def give_back(pos_part):
        cosines, sines = wave_tables(pos_part, wavevectors)
        return (general_exact(filt_cos, cosines) + general_exact(filt_sin, sines), general_exact(back_cos, cosines) + general_exact(back_sin, sines))

    long_groups, back_groups = lax.map(give_back, pos_groups)
    long_range = long_groups.transpose(1, 0, 2).reshape(channels, atoms_total)
    back_long = back_groups.transpose(1, 0, 2).reshape(channels, atoms_total)

    block_count = atoms_total // BLOCK
    blocks = features.reshape(channels, block_count, BLOCK)
    coord_blocks = positions.reshape(3, block_count, BLOCK)
    flat_ids = neighbour_ids.reshape(-1).astype(jnp.int32)
    nearby_feat = jnp.take(blocks, flat_ids, axis=1).reshape(channels, block_count, SLOTS, BLOCK)
    nearby_coord = jnp.take(coord_blocks, flat_ids, axis=1).reshape(3, block_count, SLOTS, BLOCK)
    live_mask = (jnp.arange(SLOTS, dtype=jnp.int32)[None, :] < live_counts[:, None]).astype(jnp.float32)
    weights = pair_weights(coord_blocks, nearby_coord, radial_rates, block_count, live_mask)
    gathered = jnp.einsum('cosj,rosij->rcoi', nearby_feat, weights, precision=lax.Precision.HIGHEST)
    short_range = jnp.einsum('rdc,rdoi->coi', radial_mix, gathered, precision=lax.Precision.HIGHEST).reshape(channels, atoms_total)
    layer_out = features + long_range + short_range
    back_mix = jnp.einsum('rdc,coi->rdoi', radial_mix, cotangent.reshape(channels, block_count, BLOCK), precision=lax.Precision.HIGHEST)
    contribution = jnp.einsum('rosij,rdoi->dosj', weights, back_mix, precision=lax.Precision.HIGHEST)
    back_short = jnp.zeros((channels, block_count, BLOCK), jnp.float32).at[:, flat_ids, :].add(contribution.reshape(channels, block_count * SLOTS, BLOCK))
    grad_features = cotangent + back_long + back_short.reshape(channels, atoms_total)
    return layer_out, grad_features, grad_filter
```

```python
import functools

import jax
import jax.numpy as jnp
from jax import lax
from jax.experimental import pallas as pl
from jax.experimental.pallas import tpu as pltpu
from jax.sharding import PartitionSpec as P

BLOCK = 128
REACH = 2
SLOTS = 5
ROWS = 16
LAG = 4
VMEM_LIMIT = 56 * 1024 * 1024

SIN_ROOT = (4.442867903032313, -7.30744342132285, 3.594788078837099, -0.7843740317416608)
COS_ROOT = (1.414204080468759, -6.977642056819178, 5.715238395225206, -1.7283486634852898)
SIN_HALF = (3.141592640130707, -5.167710083507862, 2.550077523214134, -0.5982912856178576, 0.0776576603009221)


def horner(coefs, z):
    value = coefs[-1]
    for coef in coefs[-2::-1]:
        value = value * z + coef
    return value


def split(x):
    high = x.astype(jnp.bfloat16)
    return high, (x - high.astype(jnp.float32)).astype(jnp.bfloat16)


def dot3(left, right, dims):
    def one(a, b):
        return lax.dot_general(a, b, (dims, ((), ())), preferred_element_type=jnp.float32)

    return one(left[0], right[0]) + (one(left[0], right[1]) + one(left[1], right[0]))


NN = ((1,), (0,))
NT = ((1,), (1,))
TN = ((0,), (0,))


def short_range(total_blocks, near, far, cols_ref, small, mix_ref, rate_ref, store):
    window = near[0].shape[1]
    own = small.shape[1]
    lengths = (total_blocks / jnp.pi, 2.0 / jnp.pi, 2.0 / jnp.pi)
    reach = window - own + BLOCK
    slots = reach // BLOCK
    base = cols_ref.shape[1] - 16
    for b in range(own // BLOCK):
        mine = slice(b * BLOCK, (b + 1) * BLOCK)
        around = slice(b * BLOCK, b * BLOCK + reach)
        squares = []
        for t in range(slots):
            rows = slice((b + t) * BLOCK, (b + t + 1) * BLOCK)
            total = None
            for d in range(3):
                turn = small[d : d + 1, mine] - cols_ref[rows, base + d : base + d + 1]
                r = turn - jnp.round(turn)
                term = (lengths[d] * (r * horner(SIN_HALF, r * r))) ** 2
                total = term if total is None else total + term
            squares.append(total)
        short = None
        for n in range(mix_ref.shape[0]):
            rate = rate_ref[n]
            ahead, behind = [], []
            for t in range(slots):
                rows = slice((b + t) * BLOCK, (b + t + 1) * BLOCK)
                at = base + 8 + slots - 1 - t
                weight = jnp.exp(-rate * squares[t])
                ahead.append(weight * small[8 + t : 9 + t, mine])
                behind.append(weight * cols_ref[rows, at : at + 1])
            gathered = dot3([x[:, around] for x in near], split(jnp.concatenate(ahead, axis=0)), NN)
            returned = dot3([x[:, around] for x in far], split(jnp.concatenate(behind, axis=0)), NN)
            mix = split(mix_ref[n])
            forth = dot3(mix, split(gathered), TN)
            back = dot3(mix, split(returned), NN)
            short = (forth, back) if short is None else (short[0] + forth, short[1] + back)
        store[0, :, mine] = short[0]
        store[1, :, mine] = short[1]


def bits_of(count):
    return [1 << k for k in range(count.bit_length() - 1)]


def layer_kernel(
    n, m, total_blocks, scale,
    feat_ref, cot_ref, pos_ref, wave_ref, filt_ref, mix_ref, rate_ref, ids_ref, live_ref,
    layer_ref, cotgrad_ref, grad_ref,
    mine, halo, nh, nl, xh, xl, cols_ref, shorts, out_ref, out_in,
    waves, turned, cots, ft, ct, th, tl, held, pair_in, halves_in, full,
    h_send, h_recv, o_send, o_recv, z_send, z_recv, c_send, c_recv, r_send, r_recv, g_send, g_recv, k_send, k_recv,
):
    atom = lax.axis_index("atom")
    mode = lax.axis_index("mode")
    channels, atoms = feat_ref.shape
    own = cot_ref.shape[1]
    tile = held.shape[3]
    bits = bits_of(n)
    core, rest = bits[0], bits[1:]
    orders = (rest, rest[::-1])
    signs = {bit: 1 - 2 * ((atom // bit) % 2) for bit in bits}

    def at(e):
        place = atom
        for bit in bits:
            if e & bit:
                place = place + signs[bit] * bit
        return place

    def share_of(ref, e):
        if len(ref.shape) == 3:
            return ref.at[at(e)]
        return ref.at[:, pl.ds(pl.multiple_of(at(e) * tile, tile), tile)]

    def remote(src, dst, send, recv, where):
        return pltpu.make_async_remote_copy(
            src_ref=src, dst_ref=dst, send_sem=send, recv_sem=recv, device_id=where, device_id_type=pl.DeviceIdType.MESH
        )

    def along(k):
        target = lax.rem(atom * m + mode + k + n * m, n * m)
        return {"atom": target // m, "mode": lax.rem(target, m)}

    sent = []

    def launch(copy):
        copy.start()
        sent.append(copy)

    steps = -(-REACH * BLOCK // own)
    shifts = [k for k in range(-steps, steps + 1) if k]
    peers = [{"atom": at(bit)} for bit in bits] + [{"mode": lax.rem(mode + r, m)} for r in range(1, m)]
    peers += [along(k) for k in shifts]
    barrier = pltpu.get_barrier_semaphore()
    for peer in peers:
        pl.semaphore_signal(barrier, inc=1, device_id=peer, device_id_type=pl.DeviceIdType.MESH)
    turned[...] = cot_ref[...].T
    pl.semaphore_wait(barrier, len(peers))

    gathers = []
    for r in range(1, m):
        gathers.append(remote(turned, cots.at[r - 1], z_send.at[r - 1], z_recv.at[r - 1], {"mode": lax.rem(mode + r, m)}))
        launch(gathers[-1])

    own_cols = pl.ds(pl.multiple_of(mode * own, own), own)
    mine[:channels, :] = feat_ref[:, own_cols]
    mine[channels : 2 * channels, :] = cot_ref[...]
    small_rows = 2 * channels
    mine[small_rows:, :] = jnp.zeros((16, own), jnp.float32)
    mine[small_rows : small_rows + 3, :] = pos_ref[:, own_cols]
    first_own = (atom * m + mode) * (own // BLOCK)
    for b in range(own // BLOCK):
        offsets = [lax.rem(ids_ref[b, t] - first_own - b + REACH + 2 * total_blocks, total_blocks) for t in range(SLOTS)]
        for o in range(SLOTS):
            value = jnp.float32(0.0)
            for t in range(SLOTS):
                value += jnp.where((offsets[t] == o) & (t < live_ref[b]), 1.0, 0.0)
            mine[small_rows + 8 + o : small_rows + 9 + o, b * BLOCK : (b + 1) * BLOCK] = jnp.full((1, BLOCK), value)
    halos = [
        remote(mine, halo.at[slot], h_send.at[slot], h_recv.at[slot], along(-k)) for slot, k in enumerate(shifts)
    ]

    def neighbourhood():
        for copy in halos:
            copy.wait_recv()
        pieces = [halo[slot] for slot in range(steps)] + [mine[...]] + [halo[slot] for slot in range(steps, 2 * steps)]
        spare = steps * own - REACH * BLOCK
        width = own + 2 * REACH * BLOCK
        near = jnp.concatenate([x[:channels] for x in pieces], axis=1)[:, spare : spare + width]
        far = jnp.concatenate([x[channels : 2 * channels] for x in pieces], axis=1)[:, spare : spare + width]
        nh[...], nl[...] = split(near)
        xh[...], xl[...] = split(far)
        last = jnp.concatenate([x[small_rows + 16 - BLOCK :] for x in pieces], axis=1)[:, spare : spare + width]
        for b in range(width // BLOCK):
            part_cols = slice(b * BLOCK, (b + 1) * BLOCK)
            cols_ref[part_cols, :] = last[:, part_cols].T
        short_range(
            total_blocks, (nh, nl), (xh, xl), cols_ref, mine[small_rows:, :], mix_ref, rate_ref, shorts
        )

    for b in range(waves.shape[0] // BLOCK):
        rows = slice(b * BLOCK, (b + 1) * BLOCK)
        wide = jnp.concatenate([wave_ref[:, rows].astype(jnp.float32), jnp.zeros((5, BLOCK), jnp.float32)], axis=0)
        waves[rows, :8] = wide.T

    def trig_rows(e, first, step):
        rows = pl.multiple_of(step * ROWS, ROWS)
        wave = waves[pl.ds(pl.multiple_of(first + step * ROWS, ROWS), ROWS), :]
        turns = (
            wave[:, 0:1] * pos_ref[0:1, :] + wave[:, 1:2] * pos_ref[1:2, :] + wave[:, 2:3] * pos_ref[2:3, :]
        )
        r = turns - jnp.round(turns)
        z = r * r
        s = r * horner(SIN_ROOT, z)
        c = horner(COS_ROOT, z)
        upper, lower = pl.ds(rows, ROWS), pl.ds(tile + rows, ROWS)
        th[e, upper, :], tl[e, upper, :] = split(1.0 - s * s)
        th[e, lower, :], tl[e, lower, :] = split(s * c)

    slices = 4
    depth = atoms // slices
    count = tile // ROWS // slices

    def trig(e):
        first = at(e) * tile

        @pl.loop(0, slices)
        def _(j):
            for i in range(count):
                trig_rows(e, first, j * count + i)

    def work(sums, following):
        for g, e in sums:
            for k in range(2):
                held[e, g, k] = jnp.zeros((tile, channels), jnp.float32)
        first = None if following is None else at(following) * tile

        @pl.loop(0, slices)
        def _(j):
            cols = pl.ds(pl.multiple_of(j * depth, depth), depth)
            for g, e in sums:
                right = (ft, ct)[g]
                both = jnp.dot(th[e, :, cols], right[cols, :], preferred_element_type=jnp.float32)
                low = jnp.dot(tl[e, :, cols], right[cols, :channels], preferred_element_type=jnp.float32)
                total = both[:, :channels] + (both[:, channels:] + low)
                for k in range(2):
                    held[e, g, k] += total[k * tile : (k + 1) * tile]
            if following is not None:
                for i in range(count):
                    trig_rows(following, first, j * count + i)

    def place(target, rows, value):
        high, low = split(value)
        target[rows, :channels] = high
        target[rows, channels:] = low

    evens = [e for e in range(n - 2, -1, -2)]
    sequence = [t for e in evens for t in (e + 1, e)]
    trig(sequence[0])
    for q in range(m):
        cols = slice(q * own, (q + 1) * own)
        place(ft, cols, feat_ref[:, cols].T)

    landing = {}
    for g in range(2):
        for k in range(2):
            live = evens
            for s, bit in enumerate(orders[k]):
                for e in live:
                    if not e & bit:
                        landing[g, k, s, e] = len(landing)
                live = [e for e in live if not e & bit]

    def stage_copy(g, k, s, e):
        bit = orders[k][s]
        slot = landing[g, k, s, e & ~bit]
        return remote(held.at[e | bit, g, k], halves_in.at[slot], r_send.at[slot], r_recv.at[slot], {"atom": at(bit)})

    def advance(g, k, e):
        for s, bit in enumerate(orders[k]):
            copy = stage_copy(g, k, s, e)
            if e & bit:
                launch(copy)
                return
            copy.wait_recv()
            held[e, g, k] += halves_in[landing[g, k, s, e]]

    across = {}
    later = []

    def catch_up():
        while later:
            advance(*later.pop(0))

    def reduced(g, e):
        if e & core:
            slot = g * (n // 2) + e // 2
            across[g, e] = remote(held.at[e, g], pair_in.at[e // 2, g], c_send.at[slot], c_recv.at[slot], {"atom": at(core)})
            launch(across[g, e])
            return
        across[g, e | core].wait_recv()
        held[e, g] += pair_in[e // 2, g]
        for k in range(2):
            if rest and e & orders[k][0]:
                advance(g, k, e)
            else:
                later.append((g, k, e))

    lag = LAG
    for number in range(n + lag):
        if number == lag:
            place(ct, pl.ds(pl.multiple_of(mode * own, own), own), turned[...])
            for r in range(1, m):
                gathers[r - 1].wait_recv()
                sender = lax.rem(mode - r + m, m)
                place(ct, pl.ds(pl.multiple_of(sender * own, own), own), cots[r - 1])
            for copy in halos:
                launch(copy)
        sums = []
        if number < n:
            sums.append((0, sequence[number]))
        if number >= lag:
            sums.append((1, sequence[number - lag]))
        work(sums, sequence[number + 1] if number + 1 < n else None)
        waiting = later[:]
        later.clear()
        for g, e in sums:
            reduced(g, e)
        fresh = later[:]
        later.clear()
        later.extend(waiting)
        catch_up()
        later.extend(fresh)

    back = [order[::-1] for order in orders]

    def half_copy(g, k, e, bit):
        slot = (g * 2 + k) * n + (e | bit)
        return remote(full.at[e, g, k], full.at[e | bit, g, k], g_send.at[slot], g_recv.at[slot], {"atom": at(bit)})

    def last_of(k, e):
        return max(p for p, bit in enumerate(back[k]) if e & bit)

    def core_copy(g, e):
        slot = g * (n // 2) + e // 2
        return remote(full.at[e, g], full.at[e | core, g], k_send.at[slot], k_recv.at[slot], {"atom": at(core)})

    def arrive(g, k, e):
        p = last_of(k, e)
        half_copy(g, k, e & ~back[k][p], back[k][p]).wait_recv()
        for bit in back[k][p + 1 :]:
            launch(half_copy(g, k, e, bit))

    def give_back(g, e, first):
        factor = share_of(filt_ref, e)[...] * scale
        high, low = split(jnp.concatenate([factor * full[e, g, 0], factor * full[e, g, 1]], axis=1))
        left = jnp.concatenate([high, low], axis=0)
        if g == 1:
            share_of(grad_ref, e)[...] = (full[e, 0, 0] * full[e, 1, 0] + full[e, 0, 1] * full[e, 1, 1]) * scale
        for q in range(m):
            chunk = slice(q * own, (q + 1) * own)
            both = jnp.dot(left, th[e, :, chunk], preferred_element_type=jnp.float32)
            total = both[:channels] + (
                both[channels:] + jnp.dot(high, tl[e, :, chunk], preferred_element_type=jnp.float32)
            )
            if first:
                out_ref[g, q] = total
            else:
                out_ref[g, q] += total

    def begin(g):
        for k in range(2):
            full[0, g, k] = held[0, g, k].T
        for stage in range(len(rest)):
            for k in range(2):
                launch(half_copy(g, k, 0, back[k][stage]))
        launch(core_copy(g, 0))

    chunks = {}

    def finish(g):
        arrivals = sorted(
            ((k, e) for e in evens if e for k in range(2)), key=lambda x: (bin(x[1]).count("1"), last_of(*x), x[1])
        )
        waiting = 0
        arrived = set()
        for k, e in arrivals:
            arrive(g, k, e)
            arrived.add((k, e))
            if (1 - k, e) in arrived:
                launch(core_copy(g, e))
                core_copy(g, waiting).wait_recv()
                give_back(g, waiting | core, False)
                give_back(g, e, False)
                waiting = e
        core_copy(g, waiting).wait_recv()
        give_back(g, waiting | core, False)
        for r in range(1, m):
            target = lax.rem(mode + r, m)
            slot = g * (m - 1) + r - 1
            chunks[g, r] = remote(
                out_ref.at[g, target], out_in.at[g, r - 1], o_send.at[slot], o_recv.at[slot], {"mode": target}
            )
            launch(chunks[g, r])

    catch = [x for x in later if x[0] == 0]
    rest_later = [x for x in later if x[0] == 1]
    for x in catch:
        advance(*x)
    begin(0)
    for x in rest_later:
        advance(*x)
    begin(1)
    give_back(0, 0, True)
    finish(0)
    give_back(1, 0, True)
    finish(1)
    neighbourhood()
    for g, ref in ((0, layer_ref), (1, cotgrad_ref)):
        total = mine[g * channels : (g + 1) * channels, :] + shorts[g] + out_ref[g, mode]
        for r in range(1, m):
            chunks[g, r].wait_recv()
            total = total + out_in[g, r - 1]
        ref[...] = total
    for copy in sent:
        copy.wait_send()


def layer_call(features, cotangent, positions, waves, filters, radial_mix, radial_rates, ids, live, n, m):
    channels, atoms = features.shape
    modes = waves.shape[1]
    tile = modes // n
    own = cotangent.shape[1]
    steps = -(-REACH * BLOCK // own)
    window = own + 2 * REACH * BLOCK
    rows = 2 * channels + 16
    vmem = pl.BlockSpec(memory_space=pltpu.VMEM)
    smem = pl.BlockSpec(memory_space=pltpu.SMEM)
    dma = pltpu.SemaphoreType.DMA
    f32 = lambda *shape: pltpu.VMEM(shape, jnp.float32)
    b16 = lambda *shape: pltpu.VMEM(shape, jnp.bfloat16)
    slots = 4 * (n // 2 - 1)
    pair = lambda count: [dma((count,)), dma((count,))]
    return pl.pallas_call(
        functools.partial(layer_kernel, n, m, n * atoms // BLOCK, 1.0 / (n * atoms)),
        out_shape=(
            jax.ShapeDtypeStruct((channels, own), jnp.float32),
            jax.ShapeDtypeStruct((channels, own), jnp.float32),
            jax.ShapeDtypeStruct(filters.shape, jnp.float32),
        ),
        in_specs=[vmem] * 6 + [smem] * 3,
        out_specs=[vmem] * 3,
        scratch_shapes=[
            f32(rows, own), f32(2 * steps, rows, own),
            b16(channels, window), b16(channels, window), b16(channels, window), b16(channels, window),
            f32(window, BLOCK), f32(2, channels, own),
            f32(2, m, channels, own), f32(2, m - 1, channels, own),
            f32(modes, BLOCK), f32(own, channels), f32(m - 1, own, channels),
            b16(atoms, 2 * channels), b16(atoms, 2 * channels),
            b16(n, 2 * tile, atoms), b16(n, 2 * tile, atoms),
            f32(n, 2, 2, tile, channels), f32(n // 2, 2, 2, tile, channels),
            f32(slots, tile, channels), f32(n, 2, 2, channels, tile),
        ]
        + pair(2 * steps) + pair(2 * (m - 1)) + pair(m - 1) + pair(n) + pair(slots) + pair(4 * n) + pair(n),
        compiler_params=pltpu.CompilerParams(vmem_limit_bytes=VMEM_LIMIT, collective_id=0, has_side_effects=True),
        name="layer",
    )(features, cotangent, positions, waves, filters, radial_mix, radial_rates, ids, live)


def per_device(features, positions, wavevectors, mode_filter, radial_mix, radial_rates, neighbour_ids, live_counts, cotangent):
    n = lax.axis_size("atom")
    m = lax.axis_size("mode")
    channels = features.shape[0]
    width = mode_filter.shape[1] // n
    cut = width % 128 != 0
    filters = mode_filter.reshape(channels, n, width).transpose(1, 0, 2) if cut else mode_filter
    layer_out, grad_features, grad_filter = layer_call(
        features, cotangent, positions, wavevectors, filters, radial_mix, radial_rates, neighbour_ids, live_counts, n, m
    )
    if cut:
        grad_filter = grad_filter.transpose(1, 0, 2).reshape(channels, -1)
    return layer_out, grad_features, grad_filter


def solution(mesh):
    in_specs = (
        P(None, "atom"),
        P(None, "atom"),
        P(None, "mode"),
        P(None, "mode"),
        P(),
        P(),
        P(("atom", "mode"), None),
        P(("atom", "mode")),
        P(None, ("atom", "mode")),
    )
    out_specs = (P(None, ("atom", "mode")), P(None, ("atom", "mode")), P(None, "mode"))
    return jax.shard_map(per_device, mesh=mesh, in_specs=in_specs, out_specs=out_specs, check_vma=False)
```

```python
import functools

import jax
import jax.numpy as jnp
from jax import lax
from jax.experimental import pallas as pl
from jax.experimental.pallas import tpu as pltpu
from jax.sharding import PartitionSpec as P

BLOCK = 128
REACH = 2
SLOTS = 5
ROWS = 16
LAG = 8
VMEM_LIMIT = 56 * 1024 * 1024

SIN_ROOT = (4.442867903032313, -7.30744342132285, 3.594788078837099, -0.7843740317416608)
COS_ROOT = (1.414204080468759, -6.977642056819178, 5.715238395225206, -1.7283486634852898)
SIN_HALF = (3.141592640130707, -5.167710083507862, 2.550077523214134, -0.5982912856178576, 0.0776576603009221)


def horner(coefs, z):
    value = coefs[-1]
    for coef in coefs[-2::-1]:
        value = value * z + coef
    return value


def split(x):
    high = x.astype(jnp.bfloat16)
    return high, (x - high.astype(jnp.float32)).astype(jnp.bfloat16)


def dot3(left, right, dims):
    def one(a, b):
        return lax.dot_general(a, b, (dims, ((), ())), preferred_element_type=jnp.float32)

    return one(left[0], right[0]) + (one(left[0], right[1]) + one(left[1], right[0]))


NN = ((1,), (0,))
NT = ((1,), (1,))
TN = ((0,), (0,))


def short_range(total_blocks, near, far, cols_ref, small, mix_ref, rate_ref, store):
    window = near[0].shape[1]
    own = small.shape[1]
    lengths = (total_blocks / jnp.pi, 2.0 / jnp.pi, 2.0 / jnp.pi)
    reach = window - own + BLOCK
    slots = reach // BLOCK
    base = cols_ref.shape[1] - 16
    for b in range(own // BLOCK):
        mine = slice(b * BLOCK, (b + 1) * BLOCK)
        around = slice(b * BLOCK, b * BLOCK + reach)
        squares = []
        for t in range(slots):
            rows = slice((b + t) * BLOCK, (b + t + 1) * BLOCK)
            total = None
            for d in range(3):
                turn = small[d : d + 1, mine] - cols_ref[rows, base + d : base + d + 1]
                r = turn - jnp.round(turn)
                term = (lengths[d] * (r * horner(SIN_HALF, r * r))) ** 2
                total = term if total is None else total + term
            squares.append(total)
        short = None
        for n in range(mix_ref.shape[0]):
            rate = rate_ref[n]
            ahead, behind = [], []
            for t in range(slots):
                rows = slice((b + t) * BLOCK, (b + t + 1) * BLOCK)
                at = base + 8 + slots - 1 - t
                weight = jnp.exp(-rate * squares[t])
                ahead.append(weight * small[8 + t : 9 + t, mine])
                behind.append(weight * cols_ref[rows, at : at + 1])
            gathered = dot3([x[:, around] for x in near], split(jnp.concatenate(ahead, axis=0)), NN)
            returned = dot3([x[:, around] for x in far], split(jnp.concatenate(behind, axis=0)), NN)
            mix = split(mix_ref[n])
            forth = dot3(mix, split(gathered), TN)
            back = dot3(mix, split(returned), NN)
            short = (forth, back) if short is None else (short[0] + forth, short[1] + back)
        store[0, :, mine] = short[0]
        store[1, :, mine] = short[1]


def bits_of(count):
    return [1 << k for k in range(count.bit_length() - 1)]


def layer_kernel(
    n, m, total_blocks, scale,
    feat_ref, cot_ref, pos_ref, wave_ref, filt_ref, mix_ref, rate_ref, ids_ref, live_ref,
    layer_ref, cotgrad_ref, grad_ref,
    mine, halo, nh, nl, xh, xl, cols_ref, shorts, out_ref, out_in,
    waves, turned, cots, ft, ct, th, tl, held, pair_in, halves_in, full,
    h_send, h_recv, o_send, o_recv, z_send, z_recv, c_send, c_recv, r_send, r_recv, g_send, g_recv, k_send, k_recv,
):
    atom = lax.axis_index("atom")
    mode = lax.axis_index("mode")
    channels, atoms = feat_ref.shape
    own = cot_ref.shape[1]
    tile = held.shape[2] // 2
    bits = bits_of(n)
    core, rest = bits[0], bits[1:]
    orders = (rest, rest[::-1])
    signs = {bit: 1 - 2 * ((atom // bit) % 2) for bit in bits}

    def at(e):
        place = atom
        for bit in bits:
            if e & bit:
                place = place + signs[bit] * bit
        return place

    def share_of(ref, e):
        if len(ref.shape) == 3:
            return ref.at[at(e)]
        return ref.at[:, pl.ds(pl.multiple_of(at(e) * tile, tile), tile)]

    def remote(src, dst, send, recv, where):
        return pltpu.make_async_remote_copy(
            src_ref=src, dst_ref=dst, send_sem=send, recv_sem=recv, device_id=where, device_id_type=pl.DeviceIdType.MESH
        )

    def along(k):
        target = lax.rem(atom * m + mode + k + n * m, n * m)
        return {"atom": target // m, "mode": lax.rem(target, m)}

    sent = []

    def launch(copy):
        copy.start()
        sent.append(copy)

    steps = -(-REACH * BLOCK // own)
    shifts = [k for k in range(-steps, steps + 1) if k]
    peers = [{"atom": at(bit)} for bit in bits] + [{"mode": lax.rem(mode + r, m)} for r in range(1, m)]
    peers += [along(k) for k in shifts]
    barrier = pltpu.get_barrier_semaphore()
    for peer in peers:
        pl.semaphore_signal(barrier, inc=1, device_id=peer, device_id_type=pl.DeviceIdType.MESH)
    turned[...] = cot_ref[...].T
    pl.semaphore_wait(barrier, len(peers))

    gathers = []
    for r in range(1, m):
        gathers.append(remote(turned, cots.at[r - 1], z_send.at[r - 1], z_recv.at[r - 1], {"mode": lax.rem(mode + r, m)}))
        launch(gathers[-1])

    own_cols = pl.ds(pl.multiple_of(mode * own, own), own)
    mine[:channels, :] = feat_ref[:, own_cols]
    mine[channels : 2 * channels, :] = cot_ref[...]
    small_rows = 2 * channels
    mine[small_rows:, :] = jnp.zeros((16, own), jnp.float32)
    mine[small_rows : small_rows + 3, :] = pos_ref[:, own_cols]
    first_own = (atom * m + mode) * (own // BLOCK)
    for b in range(own // BLOCK):
        offsets = [lax.rem(ids_ref[b, t] - first_own - b + REACH + 2 * total_blocks, total_blocks) for t in range(SLOTS)]
        for o in range(SLOTS):
            value = jnp.float32(0.0)
            for t in range(SLOTS):
                value += jnp.where((offsets[t] == o) & (t < live_ref[b]), 1.0, 0.0)
            mine[small_rows + 8 + o : small_rows + 9 + o, b * BLOCK : (b + 1) * BLOCK] = jnp.full((1, BLOCK), value)
    halos = [
        remote(mine, halo.at[slot], h_send.at[slot], h_recv.at[slot], along(-k)) for slot, k in enumerate(shifts)
    ]

    def neighbourhood():
        for copy in halos:
            copy.wait_recv()
        pieces = [halo[slot] for slot in range(steps)] + [mine[...]] + [halo[slot] for slot in range(steps, 2 * steps)]
        spare = steps * own - REACH * BLOCK
        width = own + 2 * REACH * BLOCK
        near = jnp.concatenate([x[:channels] for x in pieces], axis=1)[:, spare : spare + width]
        far = jnp.concatenate([x[channels : 2 * channels] for x in pieces], axis=1)[:, spare : spare + width]
        nh[...], nl[...] = split(near)
        xh[...], xl[...] = split(far)
        last = jnp.concatenate([x[small_rows + 16 - BLOCK :] for x in pieces], axis=1)[:, spare : spare + width]
        for b in range(width // BLOCK):
            part_cols = slice(b * BLOCK, (b + 1) * BLOCK)
            cols_ref[part_cols, :] = last[:, part_cols].T
        short_range(
            total_blocks, (nh, nl), (xh, xl), cols_ref, mine[small_rows:, :], mix_ref, rate_ref, shorts
        )

    for b in range(waves.shape[0] // BLOCK):
        rows = slice(b * BLOCK, (b + 1) * BLOCK)
        wide = jnp.concatenate([wave_ref[:, rows].astype(jnp.float32), jnp.zeros((5, BLOCK), jnp.float32)], axis=0)
        waves[rows, :8] = wide.T

    def trig_rows(e, first, step):
        rows = pl.multiple_of(step * ROWS, ROWS)
        wave = waves[pl.ds(pl.multiple_of(first + step * ROWS, ROWS), ROWS), :]
        turns = (
            wave[:, 0:1] * pos_ref[0:1, :] + wave[:, 1:2] * pos_ref[1:2, :] + wave[:, 2:3] * pos_ref[2:3, :]
        )
        r = turns - jnp.round(turns)
        z = r * r
        s = r * horner(SIN_ROOT, z)
        c = horner(COS_ROOT, z)
        upper, lower = pl.ds(rows, ROWS), pl.ds(tile + rows, ROWS)
        th[e, upper, :], tl[e, upper, :] = split(1.0 - s * s)
        th[e, lower, :], tl[e, lower, :] = split(s * c)

    slices = 1
    depth = 2 * tile // slices
    count = tile // ROWS // slices

    def trig(e):
        first = at(e) * tile

        @pl.loop(0, slices)
        def _(j):
            for i in range(count):
                trig_rows(e, first, j * count + i)

    def work(sums, following):
        first = None if following is None else at(following) * tile

        @pl.loop(0, slices)
        def _(j):
            rows = pl.ds(pl.multiple_of(j * depth, depth), depth)
            for g, e in sums:
                right = (ft, ct)[g]
                both = jnp.dot(th[e, rows, :], right[...], preferred_element_type=jnp.float32)
                low = jnp.dot(tl[e, rows, :], right[:, :channels], preferred_element_type=jnp.float32)
                held[e, g, rows, :] = both[:, :channels] + (both[:, channels:] + low)
            if following is not None:
                for i in range(count):
                    trig_rows(following, first, j * count + i)

    def place(target, rows, value):
        high, low = split(value)
        target[rows, :channels] = high
        target[rows, channels:] = low

    evens = [e for e in range(n - 2, -1, -2)]
    sequence = [t for e in evens for t in (e + 1, e)]
    trig(sequence[0])
    for q in range(m):
        cols = slice(q * own, (q + 1) * own)
        place(ft, cols, feat_ref[:, cols].T)

    landing = {}
    for g in range(2):
        for k in range(2):
            live = evens
            for s, bit in enumerate(orders[k]):
                for e in live:
                    if not e & bit:
                        landing[g, k, s, e] = len(landing)
                live = [e for e in live if not e & bit]

    def stage_copy(g, k, s, e):
        bit = orders[k][s]
        slot = landing[g, k, s, e & ~bit]
        return remote(held.at[e | bit, g, k * tile : (k + 1) * tile], halves_in.at[slot], r_send.at[slot], r_recv.at[slot], {"atom": at(bit)})

    def advance(g, k, e):
        for s, bit in enumerate(orders[k]):
            copy = stage_copy(g, k, s, e)
            if e & bit:
                launch(copy)
                return
            copy.wait_recv()
            held[e, g, k * tile : (k + 1) * tile] += halves_in[landing[g, k, s, e]]

    across = {}
    later = []

    def catch_up():
        while later:
            advance(*later.pop(0))

    def reduced(g, e):
        if e & core:
            slot = g * (n // 2) + e // 2
            across[g, e] = remote(held.at[e, g], pair_in.at[e // 2, g], c_send.at[slot], c_recv.at[slot], {"atom": at(core)})
            launch(across[g, e])
            return
        across[g, e | core].wait_recv()
        held[e, g] += pair_in[e // 2, g]
        for k in range(2):
            if rest and e & orders[k][0]:
                advance(g, k, e)
            else:
                later.append((g, k, e))

    lag = LAG
    for number in range(n + lag):
        if number == lag:
            place(ct, pl.ds(pl.multiple_of(mode * own, own), own), turned[...])
            for r in range(1, m):
                gathers[r - 1].wait_recv()
                sender = lax.rem(mode - r + m, m)
                place(ct, pl.ds(pl.multiple_of(sender * own, own), own), cots[r - 1])
            for copy in halos:
                launch(copy)
        sums = []
        if number < n:
            sums.append((0, sequence[number]))
        if number >= lag:
            sums.append((1, sequence[number - lag]))
        work(sums, sequence[number + 1] if number + 1 < n else None)
        waiting = later[:]
        later.clear()
        for g, e in sums:
            reduced(g, e)
        fresh = later[:]
        later.clear()
        later.extend(waiting)
        catch_up()
        later.extend(fresh)

    back = [order[::-1] for order in orders]

    def half_copy(g, k, e, bit):
        slot = (g * 2 + k) * n + (e | bit)
        return remote(full.at[e, g, k], full.at[e | bit, g, k], g_send.at[slot], g_recv.at[slot], {"atom": at(bit)})

    def last_of(k, e):
        return max(p for p, bit in enumerate(back[k]) if e & bit)

    def core_copy(g, e):
        slot = g * (n // 2) + e // 2
        return remote(full.at[e, g], full.at[e | core, g], k_send.at[slot], k_recv.at[slot], {"atom": at(core)})

    def arrive(g, k, e):
        p = last_of(k, e)
        half_copy(g, k, e & ~back[k][p], back[k][p]).wait_recv()
        for bit in back[k][p + 1 :]:
            launch(half_copy(g, k, e, bit))

    def give_back(g, e, first):
        factor = share_of(filt_ref, e)[...] * scale
        high, low = split(jnp.concatenate([factor * full[e, g, 0], factor * full[e, g, 1]], axis=1))
        left = jnp.concatenate([high, low], axis=0)
        if g == 1:
            share_of(grad_ref, e)[...] = (full[e, 0, 0] * full[e, 1, 0] + full[e, 0, 1] * full[e, 1, 1]) * scale
        for q in range(m):
            chunk = slice(q * own, (q + 1) * own)
            both = jnp.dot(left, th[e, :, chunk], preferred_element_type=jnp.float32)
            total = both[:channels] + (
                both[channels:] + jnp.dot(high, tl[e, :, chunk], preferred_element_type=jnp.float32)
            )
            if first:
                out_ref[g, q] = total
            else:
                out_ref[g, q] += total

    def begin(g):
        for k in range(2):
            full[0, g, k] = held[0, g, k * tile : (k + 1) * tile].T
        for stage in range(len(rest)):
            for k in range(2):
                launch(half_copy(g, k, 0, back[k][stage]))
        launch(core_copy(g, 0))

    chunks = {}

    def finish(g):
        arrivals = sorted(
            ((k, e) for e in evens if e for k in range(2)), key=lambda x: (bin(x[1]).count("1"), last_of(*x), x[1])
        )
        waiting = 0
        arrived = set()
        for k, e in arrivals:
            arrive(g, k, e)
            arrived.add((k, e))
            if (1 - k, e) in arrived:
                launch(core_copy(g, e))
                core_copy(g, waiting).wait_recv()
                give_back(g, waiting | core, False)
                give_back(g, e, False)
                waiting = e
        core_copy(g, waiting).wait_recv()
        give_back(g, waiting | core, False)
        for r in range(1, m):
            target = lax.rem(mode + r, m)
            slot = g * (m - 1) + r - 1
            chunks[g, r] = remote(
                out_ref.at[g, target], out_in.at[g, r - 1], o_send.at[slot], o_recv.at[slot], {"mode": target}
            )
            launch(chunks[g, r])

    catch = [x for x in later if x[0] == 0]
    rest_later = [x for x in later if x[0] == 1]
    for x in catch:
        advance(*x)
    begin(0)
    for x in rest_later:
        advance(*x)
    begin(1)
    give_back(0, 0, True)
    finish(0)
    give_back(1, 0, True)
    finish(1)
    neighbourhood()
    for g, ref in ((0, layer_ref), (1, cotgrad_ref)):
        total = mine[g * channels : (g + 1) * channels, :] + shorts[g] + out_ref[g, mode]
        for r in range(1, m):
            chunks[g, r].wait_recv()
            total = total + out_in[g, r - 1]
        ref[...] = total
    for copy in sent:
        copy.wait_send()


def layer_call(features, cotangent, positions, waves, filters, radial_mix, radial_rates, ids, live, n, m):
    channels, atoms = features.shape
    modes = waves.shape[1]
    tile = modes // n
    own = cotangent.shape[1]
    steps = -(-REACH * BLOCK // own)
    window = own + 2 * REACH * BLOCK
    rows = 2 * channels + 16
    vmem = pl.BlockSpec(memory_space=pltpu.VMEM)
    smem = pl.BlockSpec(memory_space=pltpu.SMEM)
    dma = pltpu.SemaphoreType.DMA
    f32 = lambda *shape: pltpu.VMEM(shape, jnp.float32)
    b16 = lambda *shape: pltpu.VMEM(shape, jnp.bfloat16)
    slots = 4 * (n // 2 - 1)
    pair = lambda count: [dma((count,)), dma((count,))]
    return pl.pallas_call(
        functools.partial(layer_kernel, n, m, n * atoms // BLOCK, 1.0 / (n * atoms)),
        out_shape=(
            jax.ShapeDtypeStruct((channels, own), jnp.float32),
            jax.ShapeDtypeStruct((channels, own), jnp.float32),
            jax.ShapeDtypeStruct(filters.shape, jnp.float32),
        ),
        in_specs=[vmem] * 6 + [smem] * 3,
        out_specs=[vmem] * 3,
        scratch_shapes=[
            f32(rows, own), f32(2 * steps, rows, own),
            b16(channels, window), b16(channels, window), b16(channels, window), b16(channels, window),
            f32(window, BLOCK), f32(2, channels, own),
            f32(2, m, channels, own), f32(2, m - 1, channels, own),
            f32(modes, BLOCK), f32(own, channels), f32(m - 1, own, channels),
            b16(atoms, 2 * channels), b16(atoms, 2 * channels),
            b16(n, 2 * tile, atoms), b16(n, 2 * tile, atoms),
            f32(n, 2, 2 * tile, channels), f32(n // 2, 2, 2 * tile, channels),
            f32(slots, tile, channels), f32(n, 2, 2, channels, tile),
        ]
        + pair(2 * steps) + pair(2 * (m - 1)) + pair(m - 1) + pair(n) + pair(slots) + pair(4 * n) + pair(n),
        compiler_params=pltpu.CompilerParams(vmem_limit_bytes=VMEM_LIMIT, collective_id=0, has_side_effects=True),
        name="layer",
    )(features, cotangent, positions, waves, filters, radial_mix, radial_rates, ids, live)


def keep_kernel(*refs):
    count = len(refs) // 2
    for i in range(count):
        refs[count + i][...] = refs[i][...]


def keep(*arrays):
    vmem = pl.BlockSpec(memory_space=pltpu.VMEM)
    return pl.pallas_call(
        keep_kernel,
        out_shape=tuple(jax.ShapeDtypeStruct(x.shape, x.dtype) for x in arrays),
        in_specs=[vmem] * len(arrays),
        out_specs=[vmem] * len(arrays),
        name="keep",
    )(*arrays)


def per_device(features, positions, wavevectors, mode_filter, radial_mix, radial_rates, neighbour_ids, live_counts, cotangent):
    n = lax.axis_size("atom")
    m = lax.axis_size("mode")
    channels = features.shape[0]
    width = mode_filter.shape[1] // n
    cut = width % 128 != 0
    filters = mode_filter.reshape(channels, n, width).transpose(1, 0, 2) if cut else mode_filter
    layer_out, grad_features, grad_filter = layer_call(
        features, cotangent, positions, wavevectors, filters, radial_mix, radial_rates, neighbour_ids, live_counts, n, m
    )
    layer_out, grad_features, grad_filter = keep(layer_out, grad_features, grad_filter)
    if cut:
        grad_filter = grad_filter.transpose(1, 0, 2).reshape(channels, -1)
    return layer_out, grad_features, grad_filter


def solution(mesh):
    in_specs = (
        P(None, "atom"),
        P(None, "atom"),
        P(None, "mode"),
        P(None, "mode"),
        P(),
        P(),
        P(("atom", "mode"), None),
        P(("atom", "mode")),
        P(None, ("atom", "mode")),
    )
    out_specs = (P(None, ("atom", "mode")), P(None, ("atom", "mode")), P(None, "mode"))
    return jax.shard_map(per_device, mesh=mesh, in_specs=in_specs, out_specs=out_specs, check_vma=False)
```

```python
import functools

import jax
import jax.numpy as jnp
from jax import lax
from jax.experimental import pallas as pl
from jax.experimental.pallas import tpu as pltpu
from jax.sharding import PartitionSpec as P

BLOCK = 128
REACH = 2
SLOTS = 5
ROWS = 16
LAG = 8
WAIT = 4
VMEM_LIMIT = 56 * 1024 * 1024

SIN_ROOT = (4.442867903032313, -7.30744342132285, 3.594788078837099, -0.7843740317416608)
COS_ROOT = (1.414204080468759, -6.977642056819178, 5.715238395225206, -1.7283486634852898)
SIN_HALF = (3.141592640130707, -5.167710083507862, 2.550077523214134, -0.5982912856178576, 0.0776576603009221)


def horner(coefs, z):
    value = coefs[-1]
    for coef in coefs[-2::-1]:
        value = value * z + coef
    return value


def split(x):
    high = x.astype(jnp.bfloat16)
    return high, (x - high.astype(jnp.float32)).astype(jnp.bfloat16)


def dot3(left, right, dims):
    def one(a, b):
        return lax.dot_general(a, b, (dims, ((), ())), preferred_element_type=jnp.float32)

    return one(left[0], right[0]) + (one(left[0], right[1]) + one(left[1], right[0]))


NN = ((1,), (0,))
NT = ((1,), (1,))
TN = ((0,), (0,))


def short_range(total_blocks, near, far, cols_ref, small, mix_ref, rate_ref, store):
    window = near[0].shape[1]
    own = small.shape[1]
    lengths = (total_blocks / jnp.pi, 2.0 / jnp.pi, 2.0 / jnp.pi)
    reach = window - own + BLOCK
    slots = reach // BLOCK
    base = cols_ref.shape[1] - 16
    for b in range(own // BLOCK):
        mine = slice(b * BLOCK, (b + 1) * BLOCK)
        around = slice(b * BLOCK, b * BLOCK + reach)
        squares = []
        for t in range(slots):
            rows = slice((b + t) * BLOCK, (b + t + 1) * BLOCK)
            total = None
            for d in range(3):
                turn = small[d : d + 1, mine] - cols_ref[rows, base + d : base + d + 1]
                r = turn - jnp.round(turn)
                term = (lengths[d] * (r * horner(SIN_HALF, r * r))) ** 2
                total = term if total is None else total + term
            squares.append(total)
        short = None
        for n in range(mix_ref.shape[0]):
            rate = rate_ref[n]
            ahead, behind = [], []
            for t in range(slots):
                rows = slice((b + t) * BLOCK, (b + t + 1) * BLOCK)
                at = base + 8 + slots - 1 - t
                weight = jnp.exp(-rate * squares[t])
                ahead.append(weight * small[8 + t : 9 + t, mine])
                behind.append(weight * cols_ref[rows, at : at + 1])
            gathered = dot3([x[:, around] for x in near], split(jnp.concatenate(ahead, axis=0)), NN)
            returned = dot3([x[:, around] for x in far], split(jnp.concatenate(behind, axis=0)), NN)
            mix = split(mix_ref[n])
            forth = dot3(mix, split(gathered), TN)
            back = dot3(mix, split(returned), NN)
            short = (forth, back) if short is None else (short[0] + forth, short[1] + back)
        store[0, :, mine] = short[0]
        store[1, :, mine] = short[1]


def bits_of(count):
    return [1 << k for k in range(count.bit_length() - 1)]


def layer_kernel(
    n, m, total_blocks, scale,
    feat_ref, cot_ref, pos_ref, wave_ref, filt_ref, mix_ref, rate_ref, ids_ref, live_ref,
    layer_ref, cotgrad_ref, grad_ref,
    mine, halo, nh, nl, xh, xl, cols_ref, shorts, out_ref, out_in,
    waves, turned, cots, ft, ct, th, tl, held, pair_in, halves_in, full,
    h_send, h_recv, o_send, o_recv, z_send, z_recv, c_send, c_recv, r_send, r_recv, g_send, g_recv, k_send, k_recv,
):
    atom = lax.axis_index("atom")
    mode = lax.axis_index("mode")
    channels, atoms = feat_ref.shape
    own = cot_ref.shape[1]
    tile = held.shape[2] // 2
    bits = bits_of(n)
    core, rest = bits[0], bits[1:]
    orders = (rest, rest[::-1])
    signs = {bit: 1 - 2 * ((atom // bit) % 2) for bit in bits}

    def at(e):
        place = atom
        for bit in bits:
            if e & bit:
                place = place + signs[bit] * bit
        return place

    def share_of(ref, e):
        if len(ref.shape) == 3:
            return ref.at[at(e)]
        return ref.at[:, pl.ds(pl.multiple_of(at(e) * tile, tile), tile)]

    def remote(src, dst, send, recv, where):
        return pltpu.make_async_remote_copy(
            src_ref=src, dst_ref=dst, send_sem=send, recv_sem=recv, device_id=where, device_id_type=pl.DeviceIdType.MESH
        )

    def along(k):
        target = lax.rem(atom * m + mode + k + n * m, n * m)
        return {"atom": target // m, "mode": lax.rem(target, m)}

    sent = []

    def launch(copy):
        copy.start()
        sent.append(copy)

    steps = -(-REACH * BLOCK // own)
    shifts = [k for k in range(-steps, steps + 1) if k]
    peers = [{"atom": at(bit)} for bit in bits] + [{"mode": lax.rem(mode + r, m)} for r in range(1, m)]
    peers += [along(k) for k in shifts]
    barrier = pltpu.get_barrier_semaphore()
    for peer in peers:
        pl.semaphore_signal(barrier, inc=1, device_id=peer, device_id_type=pl.DeviceIdType.MESH)
    turned[...] = cot_ref[...].T
    pl.semaphore_wait(barrier, len(peers))

    gathers = []
    for r in range(1, m):
        gathers.append(remote(turned, cots.at[r - 1], z_send.at[r - 1], z_recv.at[r - 1], {"mode": lax.rem(mode + r, m)}))
        launch(gathers[-1])

    own_cols = pl.ds(pl.multiple_of(mode * own, own), own)
    mine[:channels, :] = feat_ref[:, own_cols]
    mine[channels : 2 * channels, :] = cot_ref[...]
    small_rows = 2 * channels
    mine[small_rows:, :] = jnp.zeros((16, own), jnp.float32)
    mine[small_rows : small_rows + 3, :] = pos_ref[:, own_cols]
    first_own = (atom * m + mode) * (own // BLOCK)
    for b in range(own // BLOCK):
        offsets = [lax.rem(ids_ref[b, t] - first_own - b + REACH + 2 * total_blocks, total_blocks) for t in range(SLOTS)]
        for o in range(SLOTS):
            value = jnp.float32(0.0)
            for t in range(SLOTS):
                value += jnp.where((offsets[t] == o) & (t < live_ref[b]), 1.0, 0.0)
            mine[small_rows + 8 + o : small_rows + 9 + o, b * BLOCK : (b + 1) * BLOCK] = jnp.full((1, BLOCK), value)
    halos = [
        remote(mine, halo.at[slot], h_send.at[slot], h_recv.at[slot], along(-k)) for slot, k in enumerate(shifts)
    ]

    def neighbourhood():
        for copy in halos:
            copy.wait_recv()
        pieces = [halo[slot] for slot in range(steps)] + [mine[...]] + [halo[slot] for slot in range(steps, 2 * steps)]
        spare = steps * own - REACH * BLOCK
        width = own + 2 * REACH * BLOCK
        near = jnp.concatenate([x[:channels] for x in pieces], axis=1)[:, spare : spare + width]
        far = jnp.concatenate([x[channels : 2 * channels] for x in pieces], axis=1)[:, spare : spare + width]
        nh[...], nl[...] = split(near)
        xh[...], xl[...] = split(far)
        last = jnp.concatenate([x[small_rows + 16 - BLOCK :] for x in pieces], axis=1)[:, spare : spare + width]
        for b in range(width // BLOCK):
            part_cols = slice(b * BLOCK, (b + 1) * BLOCK)
            cols_ref[part_cols, :] = last[:, part_cols].T
        short_range(
            total_blocks, (nh, nl), (xh, xl), cols_ref, mine[small_rows:, :], mix_ref, rate_ref, shorts
        )

    for b in range(waves.shape[0] // BLOCK):
        rows = slice(b * BLOCK, (b + 1) * BLOCK)
        wide = jnp.concatenate([wave_ref[:, rows].astype(jnp.float32), jnp.zeros((5, BLOCK), jnp.float32)], axis=0)
        waves[rows, :8] = wide.T

    def trig_rows(e, first, step):
        rows = pl.multiple_of(step * ROWS, ROWS)
        wave = waves[pl.ds(pl.multiple_of(first + step * ROWS, ROWS), ROWS), :]
        turns = (
            wave[:, 0:1] * pos_ref[0:1, :] + wave[:, 1:2] * pos_ref[1:2, :] + wave[:, 2:3] * pos_ref[2:3, :]
        )
        r = turns - jnp.round(turns)
        z = r * r
        s = r * horner(SIN_ROOT, z)
        c = horner(COS_ROOT, z)
        upper, lower = pl.ds(rows, ROWS), pl.ds(tile + rows, ROWS)
        th[e, upper, :], tl[e, upper, :] = split(1.0 - s * s)
        th[e, lower, :], tl[e, lower, :] = split(s * c)

    slices = 1
    depth = 2 * tile // slices
    count = tile // ROWS // slices

    def trig(e):
        first = at(e) * tile

        @pl.loop(0, slices)
        def _(j):
            for i in range(count):
                trig_rows(e, first, j * count + i)

    def work(sums, following):
        first = None if following is None else at(following) * tile

        @pl.loop(0, slices)
        def _(j):
            rows = pl.ds(pl.multiple_of(j * depth, depth), depth)
            for g, e in sums:
                right = (ft, ct)[g]
                both = jnp.dot(th[e, rows, :], right[...], preferred_element_type=jnp.float32)
                low = jnp.dot(tl[e, rows, :], right[:, :channels], preferred_element_type=jnp.float32)
                held[e, g, rows, :] = both[:, :channels] + (both[:, channels:] + low)
            if following is not None:
                for i in range(count):
                    trig_rows(following, first, j * count + i)

    def place(target, rows, value):
        high, low = split(value)
        target[rows, :channels] = high
        target[rows, channels:] = low

    evens = [e for e in range(n - 2, -1, -2)]
    sequence = [t for e in evens for t in (e + 1, e)]
    trig(sequence[0])
    for q in range(m):
        cols = slice(q * own, (q + 1) * own)
        place(ft, cols, feat_ref[:, cols].T)

    landing = {}
    for g in range(2):
        for k in range(2):
            live = evens
            for s, bit in enumerate(orders[k]):
                for e in live:
                    if not e & bit:
                        landing[g, k, s, e] = len(landing)
                live = [e for e in live if not e & bit]

    def stage_copy(g, k, s, e):
        bit = orders[k][s]
        slot = landing[g, k, s, e & ~bit]
        return remote(held.at[e | bit, g, k * tile : (k + 1) * tile], halves_in.at[slot], r_send.at[slot], r_recv.at[slot], {"atom": at(bit)})

    def advance(g, k, e):
        for s, bit in enumerate(orders[k]):
            copy = stage_copy(g, k, s, e)
            if e & bit:
                launch(copy)
                return
            copy.wait_recv()
            held[e, g, k * tile : (k + 1) * tile] += halves_in[landing[g, k, s, e]]

    across = {}
    later = []

    def reduced(g, e):
        if e & core:
            slot = g * (n // 2) + e // 2
            across[g, e] = remote(held.at[e, g], pair_in.at[e // 2, g], c_send.at[slot], c_recv.at[slot], {"atom": at(core)})
            launch(across[g, e])
            return
        across[g, e | core].wait_recv()
        held[e, g] += pair_in[e // 2, g]
        for k in range(2):
            if rest and e & orders[k][0]:
                advance(g, k, e)
            else:
                later.append((g, k, e))

    back = [order[::-1] for order in orders]

    groups = [(0, 0, channels), (1, 0, channels // 2), (1, channels // 2, channels // 2)]

    def rows_of(u):
        g, first, count = groups[u]
        return g, slice(first, first + count)

    def half_copy(u, k, e, bit):
        g, rows = rows_of(u)
        slot = (u * 2 + k) * n + (e | bit)
        return remote(
            full.at[e, g, k, rows], full.at[e | bit, g, k, rows], g_send.at[slot], g_recv.at[slot], {"atom": at(bit)}
        )

    def last_of(k, e):
        return max(p for p, bit in enumerate(back[k]) if e & bit)

    def core_copy(u, e):
        g, rows = rows_of(u)
        slot = u * (n // 2) + e // 2
        return remote(
            full.at[e, g, :, rows], full.at[e | core, g, :, rows], k_send.at[slot], k_recv.at[slot], {"atom": at(core)}
        )

    def give_back(u, e):
        g, rows = rows_of(u)
        count = groups[u][2]
        factor = share_of(filt_ref, e)[rows, :] * scale
        high, low = split(jnp.concatenate([factor * full[e, g, 0, rows], factor * full[e, g, 1, rows]], axis=1))
        left = jnp.concatenate([high, low], axis=0)
        if g == 1:
            share_of(grad_ref, e)[rows, :] = (
                full[e, 0, 0, rows] * full[e, 1, 0, rows] + full[e, 0, 1, rows] * full[e, 1, 1, rows]
            ) * scale
        for q in range(m):
            chunk = slice(q * own, (q + 1) * own)
            both = jnp.dot(left, th[e, :, chunk], preferred_element_type=jnp.float32)
            total = both[:count] + (
                both[count:] + jnp.dot(high, tl[e, :, chunk], preferred_element_type=jnp.float32)
            )
            if e == 0:
                out_ref[g, q, rows] = total
            else:
                out_ref[g, q, rows] += total

    ready = [[0] for _ in groups]
    arrived = [set() for _ in groups]
    latest = [0 for _ in groups]
    chunks = {}
    order = sorted(
        ((k, e) for e in evens if e for k in range(2)), key=lambda x: (bin(x[1]).count("1"), last_of(*x), x[1])
    )
    near_part = [x for x in order if bin(x[1]).count("1") == 1]
    far_part = [x for x in order if bin(x[1]).count("1") > 1]

    def turn(g):
        for k in range(2):
            full[0, g, k] = held[0, g, k * tile : (k + 1) * tile].T

    def begin(u):
        for stage in range(len(rest)):
            for k in range(2):
                launch(half_copy(u, k, 0, back[k][stage]))
        launch(core_copy(u, 0))

    def take(u, items):
        for k, e in items:
            p = last_of(k, e)
            half_copy(u, k, e & ~back[k][p], back[k][p]).wait_recv()
            for bit in back[k][p + 1 :]:
                launch(half_copy(u, k, e, bit))
            arrived[u].add((k, e))
            if (1 - k, e) in arrived[u]:
                launch(core_copy(u, e))
                ready[u] += [latest[u] | core, e]
                latest[u] = e

    def flush(u):
        for e in ready[u]:
            if e & core:
                core_copy(u, e & ~core).wait_recv()
            give_back(u, e)
        ready[u].clear()

    def finish(u):
        ready[u].append(latest[u] | core)
        flush(u)
        g, rows = rows_of(u)
        for r in range(1, m):
            target = lax.rem(mode + r, m)
            slot = u * (m - 1) + r - 1
            chunks[u, r] = remote(
                out_ref.at[g, target, rows], out_in.at[g, r - 1, rows], o_send.at[slot], o_recv.at[slot], {"mode": target}
            )
            launch(chunks[u, r])

    pairs, fresh = [], []
    lag = LAG
    for number in range(n + lag):
        if number == lag:
            place(ct, pl.ds(pl.multiple_of(mode * own, own), own), turned[...])
            for r in range(1, m):
                gathers[r - 1].wait_recv()
                sender = lax.rem(mode - r + m, m)
                place(ct, pl.ds(pl.multiple_of(sender * own, own), own), cots[r - 1])
            for copy in halos:
                launch(copy)
        sums = []
        if number < n:
            sums.append((0, sequence[number]))
        if number >= lag:
            sums.append((1, sequence[number - lag]))
        work(sums, sequence[number + 1] if number + 1 < n else None)
        behind, pairs[:] = pairs[:], []
        for g, e in sums:
            if g and not e & core:
                pairs.append((g, e))
            else:
                reduced(g, e)
        for g, e in behind:
            reduced(g, e)
        for x in fresh:
            advance(*x)
        fresh = [x for x in later if x[2]]
        later[:] = [x for x in later if not x[2]]
        if number == n - 1 + WAIT:
            for x in later:
                if not x[0]:
                    advance(*x)
            later[:] = [x for x in later if x[0]]
            turn(0)
            begin(0)
    for g, e in pairs:
        reduced(g, e)
    early = fresh + [x for x in later if x[2]]
    final = [x for x in later if not x[2]]
    for x in early:
        advance(*x)
    flush(0)
    take(0, near_part)
    for x in final:
        advance(*x)
    turn(1)
    begin(1)
    begin(2)
    flush(0)
    take(0, far_part)
    finish(0)
    take(1, near_part)
    flush(1)
    take(2, near_part)
    take(1, far_part)
    finish(1)
    flush(2)
    take(2, far_part)
    finish(2)
    neighbourhood()
    for u in range(len(groups)):
        g, rows = rows_of(u)
        first, count = groups[u][1:]
        total = mine[g * channels + first : g * channels + first + count, :] + shorts[g, rows] + out_ref[g, mode, rows]
        for r in range(1, m):
            chunks[u, r].wait_recv()
            total = total + out_in[g, r - 1, rows]
        (layer_ref, cotgrad_ref)[g][rows, :] = total
    for copy in sent:
        copy.wait_send()


def layer_call(features, cotangent, positions, waves, filters, radial_mix, radial_rates, ids, live, n, m):
    channels, atoms = features.shape
    modes = waves.shape[1]
    tile = modes // n
    own = cotangent.shape[1]
    steps = -(-REACH * BLOCK // own)
    window = own + 2 * REACH * BLOCK
    rows = 2 * channels + 16
    vmem = pl.BlockSpec(memory_space=pltpu.VMEM)
    smem = pl.BlockSpec(memory_space=pltpu.SMEM)
    dma = pltpu.SemaphoreType.DMA
    f32 = lambda *shape: pltpu.VMEM(shape, jnp.float32)
    b16 = lambda *shape: pltpu.VMEM(shape, jnp.bfloat16)
    slots = 4 * (n // 2 - 1)
    pair = lambda count: [dma((count,)), dma((count,))]
    return pl.pallas_call(
        functools.partial(layer_kernel, n, m, n * atoms // BLOCK, 1.0 / (n * atoms)),
        out_shape=(
            jax.ShapeDtypeStruct((channels, own), jnp.float32),
            jax.ShapeDtypeStruct((channels, own), jnp.float32),
            jax.ShapeDtypeStruct(filters.shape, jnp.float32),
        ),
        in_specs=[vmem] * 6 + [smem] * 3,
        out_specs=[vmem] * 3,
        scratch_shapes=[
            f32(rows, own), f32(2 * steps, rows, own),
            b16(channels, window), b16(channels, window), b16(channels, window), b16(channels, window),
            f32(window, BLOCK), f32(2, channels, own),
            f32(2, m, channels, own), f32(2, m - 1, channels, own),
            f32(modes, BLOCK), f32(own, channels), f32(m - 1, own, channels),
            b16(atoms, 2 * channels), b16(atoms, 2 * channels),
            b16(n, 2 * tile, atoms), b16(n, 2 * tile, atoms),
            f32(n, 2, 2 * tile, channels), f32(n // 2, 2, 2 * tile, channels),
            f32(slots, tile, channels), f32(n, 2, 2, channels, tile),
        ]
        + pair(2 * steps) + pair(3 * (m - 1)) + pair(m - 1) + pair(n) + pair(slots) + pair(6 * n) + pair(3 * n // 2),
        compiler_params=pltpu.CompilerParams(vmem_limit_bytes=VMEM_LIMIT, collective_id=0, has_side_effects=True),
        name="layer",
    )(features, cotangent, positions, waves, filters, radial_mix, radial_rates, ids, live)


def keep_kernel(*refs):
    count = len(refs) // 2
    for i in range(count):
        refs[count + i][...] = refs[i][...]


def keep(*arrays):
    vmem = pl.BlockSpec(memory_space=pltpu.VMEM)
    return pl.pallas_call(
        keep_kernel,
        out_shape=tuple(jax.ShapeDtypeStruct(x.shape, x.dtype) for x in arrays),
        in_specs=[vmem] * len(arrays),
        out_specs=[vmem] * len(arrays),
        name="keep",
    )(*arrays)


def per_device(features, positions, wavevectors, mode_filter, radial_mix, radial_rates, neighbour_ids, live_counts, cotangent):
    n = lax.axis_size("atom")
    m = lax.axis_size("mode")
    channels = features.shape[0]
    width = mode_filter.shape[1] // n
    cut = width % 128 != 0
    filters = mode_filter.reshape(channels, n, width).transpose(1, 0, 2) if cut else mode_filter
    layer_out, grad_features, grad_filter = layer_call(
        features, cotangent, positions, wavevectors, filters, radial_mix, radial_rates, neighbour_ids, live_counts, n, m
    )
    layer_out, grad_features, grad_filter = keep(layer_out, grad_features, grad_filter)
    if cut:
        grad_filter = grad_filter.transpose(1, 0, 2).reshape(channels, -1)
    return layer_out, grad_features, grad_filter


def solution(mesh):
    in_specs = (
        P(None, "atom"),
        P(None, "atom"),
        P(None, "mode"),
        P(None, "mode"),
        P(),
        P(),
        P(("atom", "mode"), None),
        P(("atom", "mode")),
        P(None, ("atom", "mode")),
    )
    out_specs = (P(None, ("atom", "mode")), P(None, ("atom", "mode")), P(None, "mode"))
    return jax.shard_map(per_device, mesh=mesh, in_specs=in_specs, out_specs=out_specs, check_vma=False)
```

```python
import functools

import jax
import jax.numpy as jnp
from jax import lax
from jax.experimental import pallas as pl
from jax.experimental.pallas import tpu as pltpu
from jax.sharding import PartitionSpec as P

BLOCK = 128
REACH = 2
SLOTS = 5
ROWS = 16
LAG = 8
WAIT = 4
VMEM_LIMIT = 56 * 1024 * 1024

SIN_ROOT = (4.442867903032313, -7.30744342132285, 3.594788078837099, -0.7843740317416608)
COS_ROOT = (1.414204080468759, -6.977642056819178, 5.715238395225206, -1.7283486634852898)
SIN_HALF = (3.141592640130707, -5.167710083507862, 2.550077523214134, -0.5982912856178576, 0.0776576603009221)


def horner(coefs, z):
    value = coefs[-1]
    for coef in coefs[-2::-1]:
        value = value * z + coef
    return value


def split(x):
    high = x.astype(jnp.bfloat16)
    return high, (x - high.astype(jnp.float32)).astype(jnp.bfloat16)


def dot3(left, right, dims):
    def one(a, b):
        return lax.dot_general(a, b, (dims, ((), ())), preferred_element_type=jnp.float32)

    return one(left[0], right[0]) + (one(left[0], right[1]) + one(left[1], right[0]))


NN = ((1,), (0,))
NT = ((1,), (1,))
TN = ((0,), (0,))


def short_range(total_blocks, near, far, cols_ref, small, mix_ref, rate_ref, store):
    window = near[0].shape[1]
    own = small.shape[1]
    lengths = (total_blocks / jnp.pi, 2.0 / jnp.pi, 2.0 / jnp.pi)
    reach = window - own + BLOCK
    slots = reach // BLOCK
    base = cols_ref.shape[1] - 16
    for b in range(own // BLOCK):
        mine = slice(b * BLOCK, (b + 1) * BLOCK)
        around = slice(b * BLOCK, b * BLOCK + reach)
        squares = []
        for t in range(slots):
            rows = slice((b + t) * BLOCK, (b + t + 1) * BLOCK)
            total = None
            for d in range(3):
                turn = small[d : d + 1, mine] - cols_ref[rows, base + d : base + d + 1]
                r = turn - jnp.round(turn)
                term = (lengths[d] * (r * horner(SIN_HALF, r * r))) ** 2
                total = term if total is None else total + term
            squares.append(total)
        short = None
        for n in range(mix_ref.shape[0]):
            rate = rate_ref[n]
            ahead, behind = [], []
            for t in range(slots):
                rows = slice((b + t) * BLOCK, (b + t + 1) * BLOCK)
                at = base + 8 + slots - 1 - t
                weight = jnp.exp(-rate * squares[t])
                ahead.append(weight * small[8 + t : 9 + t, mine])
                behind.append(weight * cols_ref[rows, at : at + 1])
            gathered = dot3([x[:, around] for x in near], split(jnp.concatenate(ahead, axis=0)), NN)
            returned = dot3([x[:, around] for x in far], split(jnp.concatenate(behind, axis=0)), NN)
            mix = split(mix_ref[n])
            forth = dot3(mix, split(gathered), TN)
            back = dot3(mix, split(returned), NN)
            short = (forth, back) if short is None else (short[0] + forth, short[1] + back)
        store[0, :, mine] = short[0]
        store[1, :, mine] = short[1]


def bits_of(count):
    return [1 << k for k in range(count.bit_length() - 1)]


def layer_kernel(
    n, m, total_blocks, scale,
    feat_ref, cot_ref, pos_ref, wave_ref, filt_any, mix_any, rate_ref, ids_ref, live_ref,
    layer_ref, cotgrad_ref, grad_ref,
    mine, halo, nh, nl, xh, xl, cols_ref, shorts, out_ref, out_in,
    waves, turned, cots, ft, ct, th, tl, held, pair_in, halves_in, full,
    filt_ref, mix_ref, late, h_send, h_recv, o_send, o_recv, z_send, z_recv, c_send, c_recv, r_send, r_recv, g_send, g_recv, k_send, k_recv,
):
    atom = lax.axis_index("atom")
    mode = lax.axis_index("mode")
    channels, atoms = feat_ref.shape
    own = cot_ref.shape[1]
    tile = held.shape[2] // 2
    bits = bits_of(n)
    core, rest = bits[0], bits[1:]
    orders = (rest, rest[::-1])
    signs = {bit: 1 - 2 * ((atom // bit) % 2) for bit in bits}

    def at(e):
        place = atom
        for bit in bits:
            if e & bit:
                place = place + signs[bit] * bit
        return place

    def share_of(ref, e):
        if len(ref.shape) == 3:
            return ref.at[at(e)]
        return ref.at[:, pl.ds(pl.multiple_of(at(e) * tile, tile), tile)]

    def remote(src, dst, send, recv, where):
        return pltpu.make_async_remote_copy(
            src_ref=src, dst_ref=dst, send_sem=send, recv_sem=recv, device_id=where, device_id_type=pl.DeviceIdType.MESH
        )

    def along(k):
        target = lax.rem(atom * m + mode + k + n * m, n * m)
        return {"atom": target // m, "mode": lax.rem(target, m)}

    fetches = [
        pltpu.make_async_copy(filt_any, filt_ref, late.at[0]),
        pltpu.make_async_copy(mix_any, mix_ref, late.at[1]),
    ]
    for copy in fetches:
        copy.start()
    sent = []

    def launch(copy):
        copy.start()
        sent.append(copy)

    steps = -(-REACH * BLOCK // own)
    shifts = [k for k in range(-steps, steps + 1) if k]
    peers = [{"atom": at(bit)} for bit in bits] + [{"mode": lax.rem(mode + r, m)} for r in range(1, m)]
    peers += [along(k) for k in shifts]
    barrier = pltpu.get_barrier_semaphore()
    for peer in peers:
        pl.semaphore_signal(barrier, inc=1, device_id=peer, device_id_type=pl.DeviceIdType.MESH)
    turned[...] = cot_ref[...].T

    own_cols = pl.ds(pl.multiple_of(mode * own, own), own)
    mine[:channels, :] = feat_ref[:, own_cols]
    mine[channels : 2 * channels, :] = cot_ref[...]
    small_rows = 2 * channels
    mine[small_rows:, :] = jnp.zeros((16, own), jnp.float32)
    mine[small_rows : small_rows + 3, :] = pos_ref[:, own_cols]
    first_own = (atom * m + mode) * (own // BLOCK)
    for b in range(own // BLOCK):
        offsets = [lax.rem(ids_ref[b, t] - first_own - b + REACH + 2 * total_blocks, total_blocks) for t in range(SLOTS)]
        for o in range(SLOTS):
            value = jnp.float32(0.0)
            for t in range(SLOTS):
                value += jnp.where((offsets[t] == o) & (t < live_ref[b]), 1.0, 0.0)
            mine[small_rows + 8 + o : small_rows + 9 + o, b * BLOCK : (b + 1) * BLOCK] = jnp.full((1, BLOCK), value)
    halos = [
        remote(mine, halo.at[slot], h_send.at[slot], h_recv.at[slot], along(-k)) for slot, k in enumerate(shifts)
    ]

    def neighbourhood():
        for copy in halos:
            copy.wait_recv()
        pieces = [halo[slot] for slot in range(steps)] + [mine[...]] + [halo[slot] for slot in range(steps, 2 * steps)]
        spare = steps * own - REACH * BLOCK
        width = own + 2 * REACH * BLOCK
        near = jnp.concatenate([x[:channels] for x in pieces], axis=1)[:, spare : spare + width]
        far = jnp.concatenate([x[channels : 2 * channels] for x in pieces], axis=1)[:, spare : spare + width]
        nh[...], nl[...] = split(near)
        xh[...], xl[...] = split(far)
        last = jnp.concatenate([x[small_rows + 16 - BLOCK :] for x in pieces], axis=1)[:, spare : spare + width]
        for b in range(width // BLOCK):
            part_cols = slice(b * BLOCK, (b + 1) * BLOCK)
            cols_ref[part_cols, :] = last[:, part_cols].T
        short_range(
            total_blocks, (nh, nl), (xh, xl), cols_ref, mine[small_rows:, :], mix_ref, rate_ref, shorts
        )

    for b in range(waves.shape[0] // BLOCK):
        rows = slice(b * BLOCK, (b + 1) * BLOCK)
        wide = jnp.concatenate([wave_ref[:, rows].astype(jnp.float32), jnp.zeros((5, BLOCK), jnp.float32)], axis=0)
        waves[rows, :8] = wide.T

    pl.semaphore_wait(barrier, len(peers))

    gathers = []
    for r in range(1, m):
        gathers.append(remote(turned, cots.at[r - 1], z_send.at[r - 1], z_recv.at[r - 1], {"mode": lax.rem(mode + r, m)}))
        launch(gathers[-1])

    def trig_rows(e, first, step):
        rows = pl.multiple_of(step * ROWS, ROWS)
        wave = waves[pl.ds(pl.multiple_of(first + step * ROWS, ROWS), ROWS), :]
        turns = (
            wave[:, 0:1] * pos_ref[0:1, :] + wave[:, 1:2] * pos_ref[1:2, :] + wave[:, 2:3] * pos_ref[2:3, :]
        )
        r = turns - jnp.round(turns)
        z = r * r
        s = r * horner(SIN_ROOT, z)
        c = horner(COS_ROOT, z)
        upper, lower = pl.ds(rows, ROWS), pl.ds(tile + rows, ROWS)
        th[e, upper, :], tl[e, upper, :] = split(1.0 - s * s)
        th[e, lower, :], tl[e, lower, :] = split(s * c)

    slices = 1
    depth = 2 * tile // slices
    count = tile // ROWS // slices

    def trig(e):
        first = at(e) * tile

        @pl.loop(0, slices)
        def _(j):
            for i in range(count):
                trig_rows(e, first, j * count + i)

    def work(sums, following):
        first = None if following is None else at(following) * tile

        @pl.loop(0, slices)
        def _(j):
            rows = pl.ds(pl.multiple_of(j * depth, depth), depth)
            for g, e in sums:
                right = (ft, ct)[g]
                both = jnp.dot(th[e, rows, :], right[...], preferred_element_type=jnp.float32)
                low = jnp.dot(tl[e, rows, :], right[:, :channels], preferred_element_type=jnp.float32)
                held[e, g, rows, :] = both[:, :channels] + (both[:, channels:] + low)
            if following is not None:
                for i in range(count):
                    trig_rows(following, first, j * count + i)

    def place(target, rows, value):
        high, low = split(value)
        target[rows, :channels] = high
        target[rows, channels:] = low

    evens = [e for e in range(n - 2, -1, -2)]
    sequence = [t for e in evens for t in (e + 1, e)]
    trig(sequence[0])
    for q in range(m):
        cols = slice(q * own, (q + 1) * own)
        place(ft, cols, feat_ref[:, cols].T)

    landing = {}
    for g in range(2):
        for k in range(2):
            live = evens
            for s, bit in enumerate(orders[k]):
                for e in live:
                    if not e & bit:
                        landing[g, k, s, e] = len(landing)
                live = [e for e in live if not e & bit]

    def stage_copy(g, k, s, e):
        bit = orders[k][s]
        slot = landing[g, k, s, e & ~bit]
        return remote(held.at[e | bit, g, k * tile : (k + 1) * tile], halves_in.at[slot], r_send.at[slot], r_recv.at[slot], {"atom": at(bit)})

    def advance(g, k, e):
        for s, bit in enumerate(orders[k]):
            copy = stage_copy(g, k, s, e)
            if e & bit:
                launch(copy)
                return
            copy.wait_recv()
            held[e, g, k * tile : (k + 1) * tile] += halves_in[landing[g, k, s, e]]

    across = {}
    later = []

    def reduced(g, e):
        if e & core:
            slot = g * (n // 2) + e // 2
            across[g, e] = remote(held.at[e, g], pair_in.at[e // 2, g], c_send.at[slot], c_recv.at[slot], {"atom": at(core)})
            launch(across[g, e])
            return
        across[g, e | core].wait_recv()
        held[e, g] += pair_in[e // 2, g]
        for k in range(2):
            if rest and e & orders[k][0]:
                advance(g, k, e)
            else:
                later.append((g, k, e))

    back = [order[::-1] for order in orders]

    groups = [(0, 0, channels), (1, 0, channels // 2), (1, channels // 2, channels // 2)]

    def rows_of(u):
        g, first, count = groups[u]
        return g, slice(first, first + count)

    def half_copy(u, k, e, bit):
        g, rows = rows_of(u)
        slot = (u * 2 + k) * n + (e | bit)
        return remote(
            full.at[e, g, k, rows], full.at[e | bit, g, k, rows], g_send.at[slot], g_recv.at[slot], {"atom": at(bit)}
        )

    def last_of(k, e):
        return max(p for p, bit in enumerate(back[k]) if e & bit)

    def core_copy(u, e):
        g, rows = rows_of(u)
        slot = u * (n // 2) + e // 2
        return remote(
            full.at[e, g, :, rows], full.at[e | core, g, :, rows], k_send.at[slot], k_recv.at[slot], {"atom": at(core)}
        )

    def give_back(u, e):
        g, rows = rows_of(u)
        count = groups[u][2]
        factor = share_of(filt_ref, e)[rows, :] * scale
        high, low = split(jnp.concatenate([factor * full[e, g, 0, rows], factor * full[e, g, 1, rows]], axis=1))
        left = jnp.concatenate([high, low], axis=0)
        if g == 1:
            share_of(grad_ref, e)[rows, :] = (
                full[e, 0, 0, rows] * full[e, 1, 0, rows] + full[e, 0, 1, rows] * full[e, 1, 1, rows]
            ) * scale
        for q in range(m):
            chunk = slice(q * own, (q + 1) * own)
            both = jnp.dot(left, th[e, :, chunk], preferred_element_type=jnp.float32)
            total = both[:count] + (
                both[count:] + jnp.dot(high, tl[e, :, chunk], preferred_element_type=jnp.float32)
            )
            if e == 0:
                out_ref[g, q, rows] = total
            else:
                out_ref[g, q, rows] += total

    ready = [[0] for _ in groups]
    arrived = [set() for _ in groups]
    latest = [0 for _ in groups]
    chunks = {}
    order = sorted(
        ((k, e) for e in evens if e for k in range(2)), key=lambda x: (bin(x[1]).count("1"), last_of(*x), x[1])
    )
    near_part = [x for x in order if bin(x[1]).count("1") == 1]
    far_part = [x for x in order if bin(x[1]).count("1") > 1]

    def turn(g):
        for k in range(2):
            full[0, g, k] = held[0, g, k * tile : (k + 1) * tile].T

    def begin(u):
        for stage in range(len(rest)):
            for k in range(2):
                launch(half_copy(u, k, 0, back[k][stage]))
        launch(core_copy(u, 0))

    def take(u, items):
        for k, e in items:
            p = last_of(k, e)
            half_copy(u, k, e & ~back[k][p], back[k][p]).wait_recv()
            for bit in back[k][p + 1 :]:
                launch(half_copy(u, k, e, bit))
            arrived[u].add((k, e))
            if (1 - k, e) in arrived[u]:
                launch(core_copy(u, e))
                ready[u] += [latest[u] | core, e]
                latest[u] = e

    def flush(u):
        for e in ready[u]:
            if e & core:
                core_copy(u, e & ~core).wait_recv()
            give_back(u, e)
        ready[u].clear()

    def finish(u):
        ready[u].append(latest[u] | core)
        flush(u)
        g, rows = rows_of(u)
        for r in range(1, m):
            target = lax.rem(mode + r, m)
            slot = u * (m - 1) + r - 1
            chunks[u, r] = remote(
                out_ref.at[g, target, rows], out_in.at[g, r - 1, rows], o_send.at[slot], o_recv.at[slot], {"mode": target}
            )
            launch(chunks[u, r])

    pairs, fresh = [], []
    lag = LAG
    for number in range(n + lag):
        if number == lag:
            place(ct, pl.ds(pl.multiple_of(mode * own, own), own), turned[...])
            for r in range(1, m):
                gathers[r - 1].wait_recv()
                sender = lax.rem(mode - r + m, m)
                place(ct, pl.ds(pl.multiple_of(sender * own, own), own), cots[r - 1])
            for copy in halos:
                launch(copy)
        sums = []
        if number < n:
            sums.append((0, sequence[number]))
        if number >= lag:
            sums.append((1, sequence[number - lag]))
        work(sums, sequence[number + 1] if number + 1 < n else None)
        behind, pairs[:] = pairs[:], []
        for g, e in sums:
            if g and not e & core:
                pairs.append((g, e))
            else:
                reduced(g, e)
        for g, e in behind:
            reduced(g, e)
        for x in fresh:
            advance(*x)
        fresh = [x for x in later if x[2]]
        later[:] = [x for x in later if not x[2]]
        if number == n - 1 + WAIT:
            for x in later:
                if not x[0]:
                    advance(*x)
            later[:] = [x for x in later if x[0]]
            turn(0)
            begin(0)
    for g, e in pairs:
        reduced(g, e)
    early = fresh + [x for x in later if x[2]]
    final = [x for x in later if not x[2]]
    for x in early:
        advance(*x)
    for copy in fetches:
        copy.wait()
    flush(0)
    take(0, near_part)
    for x in final:
        advance(*x)
    turn(1)
    begin(1)
    begin(2)
    flush(0)
    take(0, far_part)
    finish(0)
    take(1, near_part)
    flush(1)
    take(2, near_part)
    take(1, far_part)
    finish(1)
    flush(2)
    take(2, far_part)
    finish(2)
    neighbourhood()
    for u in range(len(groups)):
        g, rows = rows_of(u)
        first, count = groups[u][1:]
        total = mine[g * channels + first : g * channels + first + count, :] + shorts[g, rows] + out_ref[g, mode, rows]
        for r in range(1, m):
            chunks[u, r].wait_recv()
            total = total + out_in[g, r - 1, rows]
        (layer_ref, cotgrad_ref)[g][rows, :] = total
    for copy in sent:
        copy.wait_send()


def layer_call(features, cotangent, positions, waves, filters, radial_mix, radial_rates, ids, live, n, m):
    channels, atoms = features.shape
    modes = waves.shape[1]
    tile = modes // n
    own = cotangent.shape[1]
    steps = -(-REACH * BLOCK // own)
    window = own + 2 * REACH * BLOCK
    rows = 2 * channels + 16
    vmem = pl.BlockSpec(memory_space=pltpu.VMEM)
    smem = pl.BlockSpec(memory_space=pltpu.SMEM)
    dma = pltpu.SemaphoreType.DMA
    f32 = lambda *shape: pltpu.VMEM(shape, jnp.float32)
    b16 = lambda *shape: pltpu.VMEM(shape, jnp.bfloat16)
    slots = 4 * (n // 2 - 1)
    pair = lambda count: [dma((count,)), dma((count,))]
    return pl.pallas_call(
        functools.partial(layer_kernel, n, m, n * atoms // BLOCK, 1.0 / (n * atoms)),
        out_shape=(
            jax.ShapeDtypeStruct((channels, own), jnp.float32),
            jax.ShapeDtypeStruct((channels, own), jnp.float32),
            jax.ShapeDtypeStruct(filters.shape, jnp.float32),
        ),
        in_specs=[vmem] * 4 + [pl.BlockSpec(memory_space=pl.ANY)] * 2 + [smem] * 3,
        out_specs=[vmem] * 3,
        scratch_shapes=[
            f32(rows, own), f32(2 * steps, rows, own),
            b16(channels, window), b16(channels, window), b16(channels, window), b16(channels, window),
            f32(window, BLOCK), f32(2, channels, own),
            f32(2, m, channels, own), f32(2, m - 1, channels, own),
            f32(modes, BLOCK), f32(own, channels), f32(m - 1, own, channels),
            b16(atoms, 2 * channels), b16(atoms, 2 * channels),
            b16(n, 2 * tile, atoms), b16(n, 2 * tile, atoms),
            f32(n, 2, 2 * tile, channels), f32(n // 2, 2, 2 * tile, channels),
            f32(slots, tile, channels), f32(n, 2, 2, channels, tile),
        ]
        + [pltpu.VMEM(filters.shape, jnp.float32), pltpu.VMEM(radial_mix.shape, jnp.float32), dma((2,))]
        + pair(2 * steps) + pair(3 * (m - 1)) + pair(m - 1) + pair(n) + pair(slots) + pair(6 * n) + pair(3 * n // 2),
        compiler_params=pltpu.CompilerParams(vmem_limit_bytes=VMEM_LIMIT, collective_id=0, has_side_effects=True),
        name="layer",
    )(features, cotangent, positions, waves, filters, radial_mix, radial_rates, ids, live)


def keep_kernel(*refs):
    count = len(refs) // 2
    for i in range(count):
        refs[count + i][...] = refs[i][...]


def keep(*arrays):
    vmem = pl.BlockSpec(memory_space=pltpu.VMEM)
    return pl.pallas_call(
        keep_kernel,
        out_shape=tuple(jax.ShapeDtypeStruct(x.shape, x.dtype) for x in arrays),
        in_specs=[vmem] * len(arrays),
        out_specs=[vmem] * len(arrays),
        name="keep",
    )(*arrays)


def per_device(features, positions, wavevectors, mode_filter, radial_mix, radial_rates, neighbour_ids, live_counts, cotangent):
    n = lax.axis_size("atom")
    m = lax.axis_size("mode")
    channels = features.shape[0]
    width = mode_filter.shape[1] // n
    cut = width % 128 != 0
    filters = mode_filter.reshape(channels, n, width).transpose(1, 0, 2) if cut else mode_filter
    layer_out, grad_features, grad_filter = layer_call(
        features, cotangent, positions, wavevectors, filters, radial_mix, radial_rates, neighbour_ids, live_counts, n, m
    )
    layer_out, grad_features, grad_filter = keep(layer_out, grad_features, grad_filter)
    if cut:
        grad_filter = grad_filter.transpose(1, 0, 2).reshape(channels, -1)
    return layer_out, grad_features, grad_filter


def solution(mesh):
    in_specs = (
        P(None, "atom"),
        P(None, "atom"),
        P(None, "mode"),
        P(None, "mode"),
        P(),
        P(),
        P(("atom", "mode"), None),
        P(("atom", "mode")),
        P(None, ("atom", "mode")),
    )
    out_specs = (P(None, ("atom", "mode")), P(None, ("atom", "mode")), P(None, "mode"))
    return jax.shard_map(per_device, mesh=mesh, in_specs=in_specs, out_specs=out_specs, check_vma=False)
```
